512 devices in a mesh: dp: 64 (over z, x), expert: 8 (over y, core).
Axes of the slice: x: 4, y: 4, z: 16, core: 2. Of those that a mesh axis runs over, the one named last changes fastest.
Arguments:
- tokens: bfloat16 [65536, 4096], P(('dp', 'expert')), may hold values from -6 to 6
- queries: bfloat16 [65536, 512], P(('dp', 'expert')), may hold values from -300 to 300
- keys: bfloat16 [65536, 512], P(('dp', 'expert')), may hold values from -5 to 5
- positions: int32 [65536], P(('dp', 'expert')), may hold values from 0 to 2046, as said below
- routes: int32 [8, 65536, 2], P(None, ('dp', 'expert')), may hold values from 0 to 7, all different within a row; in each aligned block of 1024 rows (0 to 1023, 1024 to 2047, ..., all dimensions but the last counted through in order) at most 512 rows name the same one
- router: bfloat16 [4096, 64], replicated, may hold values from -0.09375 to 0.09375
- value_experts: bfloat16 [8, 4096, 512], P('expert', 'dp'), may hold values from -0.09375 to 0.09375
Outputs:
- attended: bfloat16 [65536, 512], P(('dp', 'expert'))
The draws below stay inside these ranges and needn't reach their ends.
Inputs may be any that keep to these rules, and one draw needn't show every extreme that they name: `routes`: each head of a token names 2 different experts. For one head, no expert is named by more than 512 tokens of one sequence, and in every draw some expert is named by exactly 512. `positions`: within each sequence the ids start at 0 and rise by 1 or 2 from one token to the next; in one sequence of every draw each step is 2.
All inputs are finite; a program needn't handle non-finite values.
Results may differ from the reference program's by a relative error of at most 0.0095.
Values may be sent and summed in bfloat16 or wider, within the bound.
No kernel may reach another device: no remote copies, remote signals or barrier semaphores. Data moves between devices by JAX's collectives and lax.ppermute only.
A program may use at most 64 MiB of HBM per device.

```python
import math
import jax
import jax.numpy as jnp
import numpy as np
from jax import lax

D = 4096
H = 8
DH = 64
E = 8
TOP = 2
LEN = 1024
TOKENS = 65536
CAP = 512


def common_positions(key):
    seq_count = TOKENS // LEN
    steps_up = jax.random.randint(jax.random.fold_in(key, 7), (seq_count, LEN), 1, 3)
    full_seq = jax.random.randint(jax.random.fold_in(key, 11), (), 0, seq_count)
    seq_ids = jnp.arange(seq_count, dtype=jnp.int32)
    steps_up = jnp.where((seq_ids == full_seq)[:, None], 2, steps_up)
    pos_ids = jnp.cumsum(steps_up, axis=1) - steps_up[:, :1]
    return pos_ids.reshape(TOKENS).astype(jnp.int32)


def common_keys(key):
    return jnp.clip(jax.random.normal(jax.random.fold_in(key, 13), (TOKENS, H * DH), jnp.float32), -5.0, 5.0)


def draw_positions(key, part):
    return common_positions(key)


def draw_keys(key, part):
    return common_keys(key).astype(jnp.bfloat16)


def draw_queries(key, part):
    base = jax.random.normal(jax.random.fold_in(key, 17), (TOKENS, H * DH), jnp.float32)
    base = jnp.clip(base, -5.0, 5.0)
    return base.astype(jnp.bfloat16)


def levels(own_key, extent, split, low, high):
    loudness, own = 1.0, jax.random.fold_in(own_key, 6)
    for axis_at, blocks in split:
        heights = jnp.exp(jax.random.uniform(jax.random.fold_in(own, axis_at), (blocks,), jnp.float32, low / len(split), high / len(split)))
        loudness = loudness * jnp.repeat(heights, extent[axis_at] // blocks).reshape([-1 if axis == axis_at else 1 for axis in range(len(extent))])
    return loudness


def assign_block(stream_key, own, number, rows, amount, top, bound, skew):
    order = jax.random.permutation(stream_key, amount)
    crowded, common = load_shares(amount, rows * top, bound, skew, True), load_shares(amount, rows * top, bound, skew, False)
    places = jnp.arange(amount)

    def named(sizes, turn):
        used = int((sizes > 0).sum())
        fixed = max(1, used // 4)
        shifted = fixed + (places - fixed + turn * (used - fixed)) % max(1, amount - fixed)
        return jnp.zeros((amount,), jnp.int32).at[order[jnp.where(places < fixed, places, shifted)]].set(jnp.asarray(sizes, jnp.int32))

    sizes = jnp.where(number % 4 == 0, named(crowded, number // 4), named(common, number - number // 4 - 1))
    mixed = jax.random.permutation(jax.random.fold_in(own, 3), amount)
    source_of, receiver = mixed[0:amount // 2 * 2:2], mixed[1:amount // 2 * 2:2]
    margin = jnp.minimum(sizes[source_of] - 1, bound - sizes[receiver]) // 2
    margin = jnp.where((source_of == order[0]) | (receiver == order[0]) | (sizes[receiver] == 0), 0, jnp.maximum(margin, 0))
    shifted = jax.random.randint(jax.random.fold_in(own, 4), (amount // 2,), 0, 1 << 20) % (margin + 1)
    sizes = sizes.at[source_of].add(-shifted).at[receiver].add(shifted)
    items = jnp.searchsorted(jnp.cumsum(sizes), jnp.arange(rows * top), side="right").astype(jnp.int32)
    listing = items.reshape(top, rows).T
    listing = listing[jax.random.permutation(jax.random.fold_in(own, 1), rows)]
    turn = jax.random.randint(jax.random.fold_in(own, 2), (rows, 1), 0, top)
    return jnp.take_along_axis(listing, (jnp.arange(top)[None, :] + turn) % top, axis=1)


def load_shares(count, total, most, skew, full):
    loads = [(1 << 20) // math.isqrt(grade ** skew) + 1 for grade in range(1, count + 1)]
    largest = most if full else min(most, max(-(-total // count), total * loads[0] // sum(loads)))
    least = 1 if total - largest >= count - 1 else 0
    holding, surplus = [largest] + [least] * (count - 1), total - largest - least * (count - 1)
    while surplus > 0:
        movable = [i for i in range(1, count) if holding[i] < largest] or [i for i in range(1, count) if holding[i] < most]
        mass, remaining = sum([loads[i] for i in movable]), surplus
        for i in movable:
            more = min(most - holding[i], max(1, remaining * loads[i] // mass), surplus)
            holding[i] = holding[i] + more
            surplus = surplus - more
    return np.array(holding)


def centred(key, dims, width, bound, cuts=(), kind=jnp.bfloat16):
    drawn = jax.random.normal(key, dims, jnp.float32) * width
    if len(cuts) > 0:
        drawn = levels(key, dims, cuts, -0.22, 0.18) * drawn
    return jnp.clip(drawn, min=-bound, max=bound).astype(kind)


def setup_inputs(seed: int = 0) -> dict:
    key_list = jax.random.split(jax.random.key(seed), 8)
    tokens = centred(key_list[0], (TOKENS, D), 1.0, 6.0, ((0, 512),))
    queries = draw_queries(jax.random.fold_in(key_list[7], 71), 0)
    keys = draw_keys(jax.random.fold_in(key_list[7], 71), 0)
    positions = draw_positions(jax.random.fold_in(key_list[7], 71), 0)
    routes_keys = jax.random.split(jax.random.fold_in(key_list[4], 1), H * TOKENS // LEN)
    routes_turns = jax.random.permutation(jax.random.fold_in(key_list[4], 3), H * TOKENS // LEN)
    routes = jax.vmap(lambda own, number: assign_block(jax.random.fold_in(key_list[4], 2), own, number, LEN, E, TOP, CAP, 2))(routes_keys, routes_turns).reshape((H, TOKENS, TOP))
    router = centred(key_list[5], (D, H * E), D ** -0.5, 0.09375)
    value_experts = centred(key_list[6], (E, D, H * DH), D ** -0.5, 0.09375, ((0, 8), (1, 64)))
    return {"tokens": tokens, "queries": queries, "keys": keys, "positions": positions, "routes": routes, "router": router, "value_experts": value_experts}


rope_base = 500000.0
rope_scale = 8.0


def rotate_rope(head_vals, pos_ids):
    half_dim = head_vals.shape[-1] // 2
    inv_freq = rope_base ** (-jnp.arange(half_dim, dtype=jnp.float32) * 2.0 / head_vals.shape[-1])
    angles = pos_ids.astype(jnp.float32)[:, None] / rope_scale * inv_freq[None, :]
    cosine = jnp.cos(angles)[:, None, :]
    sine = jnp.sin(angles)[:, None, :]
    first = head_vals[..., :half_dim].astype(jnp.float32)
    second = head_vals[..., half_dim:].astype(jnp.float32)
    return jnp.concatenate([first * cosine - second * sine, second * cosine + first * sine], axis=-1).astype(jnp.bfloat16)


def sequence_values(seq_tokens, seq_routes, router, value_experts):
    seq_len = seq_tokens.shape[0]
    logits = jnp.dot(seq_tokens, router, preferred_element_type=jnp.float32)
    zero_index = jnp.zeros((), jnp.int32)

    def one_pair(pair_id):
        head_id = (pair_id // E).astype(jnp.int32)
        expert_id = (pair_id % E).astype(jnp.int32)
        head_routes = lax.dynamic_index_in_dim(seq_routes, head_id, 0, keepdims=False)
        chosen = jnp.any(head_routes == expert_id, axis=-1)
        slot_of = jnp.cumsum(chosen.astype(jnp.int32)) - 1
        target = jnp.where(chosen, slot_of, CAP).astype(jnp.int32)
        slot_index = jnp.zeros((CAP,), jnp.int32).at[target].set(jnp.arange(seq_len, dtype=jnp.int32), mode="drop")
        filled = jnp.arange(CAP, dtype=jnp.int32) < jnp.sum(chosen.astype(jnp.int32))
        gathered = seq_tokens[slot_index]
        weight_cols = lax.dynamic_slice(value_experts, (expert_id, zero_index, (head_id * DH).astype(jnp.int32)), (1, D, DH))[0]
        projected = jnp.dot(gathered, weight_cols, preferred_element_type=jnp.float32)
        gate_vals = jax.nn.sigmoid(logits[slot_index, head_id * E + expert_id])
        contrib = jnp.where(filled[:, None], gate_vals[:, None] * projected, jnp.zeros_like(projected))
        return jnp.zeros((seq_len, DH), jnp.float32).at[slot_index].add(contrib)

    pairs = lax.map(one_pair, jnp.arange(H * E, dtype=jnp.int32))
    summed = jnp.sum(pairs.reshape(H, E, seq_len, DH), axis=1)
    return jnp.transpose(summed, (1, 0, 2)).astype(jnp.bfloat16)


def one_sequence(packed):
    seq_tokens, seq_queries, seq_keys, seq_pos, seq_routes, router, value_experts = packed
    values = sequence_values(seq_tokens, seq_routes, router, value_experts)
    q_rot = rotate_rope(seq_queries, seq_pos)
    k_rot = rotate_rope(seq_keys, seq_pos)
    scores = jnp.einsum("qhd,khd->hqk", q_rot.astype(jnp.float32), k_rot.astype(jnp.float32)) * (DH ** -0.5)
    query_pos = jnp.arange(LEN, dtype=jnp.int32)
    allowed = query_pos[None, :] <= query_pos[:, None]
    scores = jnp.where(allowed[None], scores, -1e30)
    top_score = jnp.max(scores, axis=-1, keepdims=True)
    expd = jnp.exp(scores - top_score)
    weights = (expd / jnp.sum(expd, axis=-1, keepdims=True)).astype(jnp.bfloat16)
    attended = jnp.einsum("hqk,khd->qhd", weights.astype(jnp.float32), values.astype(jnp.float32))
    return attended.astype(jnp.bfloat16).reshape(LEN, H * DH)


def reference(tokens, queries, keys, positions, routes, router, value_experts):
    seq_count = TOKENS // LEN

    def run_one(packed):
        return one_sequence(packed + (router, value_experts))

    packed = (tokens.reshape(seq_count, LEN, D),
              queries.reshape(seq_count, LEN, H, DH),
              keys.reshape(seq_count, LEN, H, DH),
              positions.reshape(seq_count, LEN),
              jnp.transpose(routes.reshape(H, seq_count, LEN, TOP), (1, 0, 2, 3)))
    return lax.map(run_one, packed).reshape(TOKENS, H * DH)
```

```python
import functools

import jax
import jax.numpy as jnp
from jax import lax
from jax.experimental import pallas as pl
from jax.experimental.pallas import tpu as pltpu
from jax.sharding import Mesh
from jax.sharding import PartitionSpec as P


rope_base = 500000.0
rope_scale = 8.0
F32, BF16 = jnp.float32, jnp.bfloat16
NT = (((1,), (1,)), ((), ()))

BLOCKS = 2


def gate_rows(blocks):
    return max(64 // (blocks * blocks), 16)


def regroup_kernel(tok_ref, gate_ref, out_ref, *, sub, blocks):
    rows = tok_ref.shape[0]
    per = 128 // sub
    fine = 64 // sub
    depth = per * 128
    row = lax.broadcasted_iota(jnp.int32, (depth, 128), 0)
    col = lax.broadcasted_iota(jnp.int32, (depth, 128), 1)
    for half in range(2):
        for slot in range(per):
            pick = (row // 128 == col // sub) & (row % 128 == slot * sub + col % sub)
            pick = jnp.where(pick, 1.0, 0.0).astype(BF16)
            seq, part_of = divmod(half * per + slot, fine)
            for part in range(16 // per):
                cat = jnp.concatenate(
                    [tok_ref[:, pl.ds((part * per + i) * 256 + half * 128, 128)] for i in range(per)], axis=1
                )
                got = jnp.dot(cat, pick, preferred_element_type=F32).astype(BF16)
                for block in range(blocks):
                    out_ref[(seq * blocks + block) * fine + part_of, :rows, pl.ds(part * 128, 128)] = got
    high = gate_ref.shape[0] // (blocks * blocks)
    for block in range(blocks):
        for tile in range(blocks):
            mine = gate_ref[pl.ds((block * blocks + tile) * high, high), :].astype(BF16)
            for seq in range(4):
                for part_of in range(fine):
                    spot = (seq * blocks + block) * fine + part_of
                    out_ref[spot, rows : rows + high, pl.ds(tile * 128, 128)] = mine
                    if high < out_ref.shape[1] - rows:
                        rest = jnp.zeros((out_ref.shape[1] - rows - high, 128), BF16)
                        out_ref[spot, rows + high :, pl.ds(tile * 128, 128)] = rest


def regroup(tokens, gates, sub, blocks):
    rows, width = tokens.shape
    slices = 256 // sub
    shape = (slices * blocks, rows + gate_rows(blocks), width // slices)
    return pl.pallas_call(
        functools.partial(regroup_kernel, sub=sub, blocks=blocks),
        out_shape=jax.ShapeDtypeStruct(shape, BF16),
        cost_estimate=pl.CostEstimate(flops=1 << 31, bytes_accessed=4 << 20, transcendentals=0),
        name="regroup",
    )(tokens, gates)


def rope_kernel(q_ref, k_ref, cos_ref, sin_ref, out_ref):
    cosine, sine = cos_ref[...], sin_ref[...]
    lane = lax.broadcasted_iota(jnp.int32, cosine.shape, 1)
    low = lane % 64 < 32
    left = lane < 64

    def rot(tile):
        tile = tile.astype(F32)
        other = jnp.where(low, pltpu.roll(tile, 96, 1), pltpu.roll(tile, 32, 1))
        return (tile * cosine + other * sine).astype(BF16).astype(F32)

    for i in range(q_ref.shape[1] // 128):
        q = rot(q_ref[:, pl.ds(i * 128, 128)])
        k = rot(k_ref[:, pl.ds(i * 128, 128)])
        out_ref[2 * i] = jnp.where(left, q, pltpu.roll(k, 64, 1)).astype(BF16)
        out_ref[2 * i + 1] = jnp.where(left, pltpu.roll(q, 64, 1), k).astype(BF16)


def rope(queries, keys, positions):
    rows, width = queries.shape
    lane = jnp.arange(128, dtype=jnp.int32)
    inv_freq = rope_base ** (-(lane % 32).astype(F32) * 2.0 / 64)
    angles = positions.astype(F32)[:, None] / rope_scale * inv_freq[None, :]
    cosine = jnp.cos(angles)
    sine = jnp.where(lane % 64 < 32, -1.0, 1.0)[None, :] * jnp.sin(angles)
    return pl.pallas_call(
        rope_kernel,
        out_shape=jax.ShapeDtypeStruct((width // 64, rows, 128), BF16),
        name="rope",
    )(queries, keys, cosine, sine)


def experts_kernel(x_ref, w_ref, rest_ref, out_ref, wt_ref, *, n_e, tok_dev):
    zs, units, sub, _ = w_ref.shape
    depth = zs * sub
    tiles = (units + 1) // n_e

    @pl.when((pl.program_id(0) == 0) & (pl.program_id(1) == 0))
    def _():
        for u in range(units + 1):
            e, tile = divmod(u, tiles)
            one = w_ref[:, u] if u < units else rest_ref[:, 0]
            wt_ref[tile, pl.ds(e * 128, 128), :] = one.reshape(depth, 128).astype(F32).T.astype(BF16)

    n = x_ref.shape[0]
    x = x_ref[:, :tok_dev, :].reshape(n * tok_dev, depth)
    lanes = depth // 128
    high = 64 // (lanes * lanes)
    gates = jnp.concatenate(
        [
            jnp.concatenate(
                [x_ref[i, tok_dev:, pl.ds(t * 128, 128)].astype(F32)[:high] for t in range(lanes)], axis=0
            )
            for i in range(n)
        ],
        axis=1,
    )
    for tile in range(tiles):
        prod = lax.dot_general(wt_ref[tile], x, NT, preferred_element_type=F32)
        acc = None
        for e in range(n_e):
            gate = jnp.concatenate(
                [
                    jnp.broadcast_to(gates[h * n_e + e : h * n_e + e + 1, :], (64, n * tok_dev))
                    for h in (2 * tile, 2 * tile + 1)
                ],
                axis=0,
            )
            term = prod[e * 128 : (e + 1) * 128] * gate
            acc = term if acc is None else acc + term
        out_ref[0, pl.ds(tile * 128, 128), :] = acc.astype(BF16)


def experts(x, w, rest, seqs, n_e, tok_dev):
    blocks, rows, depth = x.shape
    units = w.shape[1] + 1
    cols = units // n_e * 128
    step = 4
    per_seq = blocks // seqs
    return pl.pallas_call(
        functools.partial(experts_kernel, n_e=n_e, tok_dev=tok_dev),
        grid=(seqs, per_seq // step),
        in_specs=[
            pl.BlockSpec((step, rows, depth), lambda s, t: (s * (per_seq // step) + t, 0, 0)),
            pl.BlockSpec(w.shape, lambda s, t: (0, 0, 0, 0)),
            pl.BlockSpec(rest.shape, lambda s, t: (0, 0, 0, 0)),
        ],
        out_specs=pl.BlockSpec((1, cols, step * tok_dev), lambda s, t: (s, 0, t)),
        out_shape=jax.ShapeDtypeStruct((seqs, cols, per_seq * tok_dev), BF16),
        scratch_shapes=[pltpu.VMEM((cols // 128, n_e * 128, depth), BF16)],
        cost_estimate=pl.CostEstimate(
            flops=2 * blocks * tok_dev * depth * n_e * cols, bytes_accessed=8 << 20, transcendentals=0
        ),
        name="experts",
    )(x, w, rest)


TILE = 256


def weights_kernel(qk_ref, out_ref):
    blocks, rows, _ = qk_ref.shape
    length = blocks * rows
    qk = qk_ref[...].reshape(length, 128)
    q, k = qk[:, :64], qk[:, 64:]
    for j in range(length // TILE):
        upto = (j + 1) * TILE
        scores = lax.dot_general(k[:upto], q[j * TILE : upto], NT, preferred_element_type=F32) * 0.125
        key = lax.broadcasted_iota(jnp.int32, scores.shape, 0)
        query = lax.broadcasted_iota(jnp.int32, scores.shape, 1) + j * TILE
        scores = jnp.where(key <= query, scores, -1e30)
        top = jnp.max(scores, axis=0, keepdims=True)
        expd = jnp.exp(scores - top)
        out_ref[j, :upto, :] = (expd / jnp.sum(expd, axis=0, keepdims=True)).astype(BF16)


def attention_weights(qk):
    blocks, rows, _ = qk.shape
    length = blocks * rows
    return pl.pallas_call(
        weights_kernel,
        out_shape=jax.ShapeDtypeStruct((length // TILE, length, TILE), BF16),
        cost_estimate=pl.CostEstimate(flops=1 << 30, bytes_accessed=4 << 20, transcendentals=1 << 20),
        name="weights",
    )(qk)


def attend_kernel(part_ref, p_ref, out_ref):
    rows = out_ref.shape[2]
    total = part_ref[0].astype(F32)
    for i in range(1, part_ref.shape[0]):
        total = total + part_ref[i].astype(F32)
    values = total.astype(BF16)
    for j in range(p_ref.shape[0]):
        upto = (j + 1) * TILE
        got = jnp.dot(values[:, :upto], p_ref[j, :upto, :], preferred_element_type=F32).astype(BF16)
        for b in range(TILE // rows):
            out_ref[j * (TILE // rows) + b] = got[:, b * rows : (b + 1) * rows]


def attend(parts, weights, blocks, rows):
    return pl.pallas_call(
        attend_kernel,
        out_shape=jax.ShapeDtypeStruct((blocks, 64, rows), BF16),
        cost_estimate=pl.CostEstimate(flops=1 << 28, bytes_accessed=4 << 20, transcendentals=0),
        name="attend",
    )(parts, weights)


def a2a(array, axes):
    return lax.all_to_all(array, axes, 0, 0, tiled=True)


def per_device(tokens, queries, keys, positions, routes, router, value_experts):
    tok_dev, width = tokens.shape
    heads = routes.shape[0]
    n_exp = router.shape[1] // heads
    yh, yl = lax.axis_size("yh"), lax.axis_size("yl")
    seqs, zs, cores = lax.axis_size("x"), lax.axis_size("z"), lax.axis_size("c")
    group = ("yh", "yl", "c")
    plane = ("x",) + group
    fine = yl * cores
    own = value_experts[0]
    sub = own.shape[0] // fine
    cols = own.shape[1] // yh
    hb = heads // yh

    pieces = own.reshape(fine, sub, yh, cols // 128, 128).transpose(2, 0, 3, 1, 4)
    mine = a2a(pieces.reshape(yh * fine, cols // 128, sub, 128), group)
    mine = mine.reshape(n_exp * cols // 128, sub, 128)
    w = lax.all_gather(mine[:-1], "z", axis=0)
    rest = a2a(jnp.broadcast_to(mine[-1:], (zs, sub, 128)), "z")[:, None]

    logits = lax.dot_general(router, tokens, (((0,), (1,)), ((), ())), preferred_element_type=F32)
    ids = jnp.arange(n_exp, dtype=jnp.int32)
    named = jnp.any(routes[:, None, :, :] == ids[None, :, None, None], axis=-1)
    gates = jnp.where(named.reshape(heads * n_exp, tok_dev), jax.nn.sigmoid(logits), 0.0)
    x = a2a(regroup(tokens, gates, sub, yh), plane)

    qk = a2a(rope(queries, keys, positions), group)

    partial = experts(x, w, rest, seqs, n_exp, tok_dev)
    partial = partial.reshape(seqs * hb, 64, partial.shape[2])
    parts = a2a(partial, ("x", "yl", "c"))
    got = attend(parts, attention_weights(qk), qk.shape[0], tok_dev)
    got = a2a(got, group)
    return got.reshape(heads * 64, tok_dev).T


def solution(mesh):
    fold = Mesh(mesh.devices.reshape(16, 4, BLOCKS, 4 // BLOCKS, 2), ("z", "x", "yh", "yl", "c"))
    rows = ("z", "x", "yh", "yl", "c")
    placed = (
        P(rows, None),
        P(rows, None),
        P(rows, None),
        P(rows),
        P(None, rows, None),
        P(),
        P(("yh", "yl", "c"), ("z", "x"), None),
    )
    return jax.shard_map(per_device, mesh=fold, in_specs=placed, out_specs=P(rows, None), check_vma=False)
```

```python
import functools

import jax
import jax.numpy as jnp
from jax import lax
from jax.experimental import pallas as pl
from jax.experimental.pallas import tpu as pltpu
from jax.sharding import Mesh
from jax.sharding import PartitionSpec as P


rope_base = 500000.0
rope_scale = 8.0
F32, BF16 = jnp.float32, jnp.bfloat16
NT = (((1,), (1,)), ((), ()))

BLOCKS = 2


def gate_rows(blocks):
    return max(64 // (blocks * blocks), 16)


def regroup_kernel(tok_ref, gate_ref, out_ref, *, sub, blocks):
    rows = tok_ref.shape[0]
    per = 128 // sub
    fine = 64 // sub
    depth = per * 128
    row = lax.broadcasted_iota(jnp.int32, (depth, 128), 0)
    col = lax.broadcasted_iota(jnp.int32, (depth, 128), 1)
    for half in range(2):
        for slot in range(per):
            pick = (row // 128 == col // sub) & (row % 128 == slot * sub + col % sub)
            pick = jnp.where(pick, 1.0, 0.0).astype(BF16)
            seq, part_of = divmod(half * per + slot, fine)
            for part in range(16 // per):
                cat = jnp.concatenate(
                    [tok_ref[:, pl.ds((i * (16 // per) + part) * 256 + half * 128, 128)] for i in range(per)], axis=1
                )
                got = jnp.dot(cat, pick, preferred_element_type=F32).astype(BF16)
                for block in range(blocks):
                    out_ref[(seq * blocks + block) * fine + part_of, :rows, pl.ds(part * 128, 128)] = got
    high = gate_ref.shape[0] // (blocks * blocks)
    for block in range(blocks):
        for tile in range(blocks):
            mine = gate_ref[pl.ds((block * blocks + tile) * high, high), :].astype(BF16)
            for seq in range(4):
                for part_of in range(fine):
                    spot = (seq * blocks + block) * fine + part_of
                    out_ref[spot, rows : rows + high, pl.ds(tile * 128, 128)] = mine
                    if high < out_ref.shape[1] - rows:
                        rest = jnp.zeros((out_ref.shape[1] - rows - high, 128), BF16)
                        out_ref[spot, rows + high :, pl.ds(tile * 128, 128)] = rest


def regroup(tokens, gates, sub, blocks):
    rows, width = tokens.shape
    slices = 256 // sub
    shape = (slices * blocks, rows + gate_rows(blocks), width // slices)
    return pl.pallas_call(
        functools.partial(regroup_kernel, sub=sub, blocks=blocks),
        out_shape=jax.ShapeDtypeStruct(shape, BF16),
        cost_estimate=pl.CostEstimate(flops=1 << 31, bytes_accessed=4 << 20, transcendentals=0),
        compiler_params=pltpu.CompilerParams(vmem_limit_bytes=16 << 20),
        name="regroup",
    )(tokens, gates)


def pack_kernel(own_ref, q_ref, k_ref, cos_ref, sin_ref, out_ref, *, blocks, sub):
    cosine, sine = cos_ref[...], sin_ref[...]
    lane = lax.broadcasted_iota(jnp.int32, cosine.shape, 1)
    low = lane % 64 < 32
    left = lane < 64
    tiles = 4 // blocks
    fine = 64 // sub
    for block in range(blocks):
        first, second = (
            own_ref[:, pl.ds((block * tiles + i) * 128, 128)].astype(F32) for i in range(2)
        )
        near = left[: first.shape[0]]
        halves = (
            jnp.where(near, first, pltpu.roll(second, 64, 1)).astype(BF16),
            jnp.where(near, pltpu.roll(first, 64, 1), second).astype(BF16),
        )
        for part in range(fine):
            for i, half in enumerate(halves):
                out_ref[block * fine + part, pl.ds(i * sub, sub), :] = half[part * sub : (part + 1) * sub]

    def rot(tile):
        tile = tile.astype(F32)
        other = jnp.where(low, pltpu.roll(tile, 96, 1), pltpu.roll(tile, 32, 1))
        return (tile * cosine + other * sine).astype(BF16).astype(F32)

    top = tiles * sub
    for i in range(q_ref.shape[1] // 128):
        q = rot(q_ref[:, pl.ds(i * 128, 128)])
        k = rot(k_ref[:, pl.ds(i * 128, 128)])
        out_ref[2 * i, top:] = jnp.where(left, q, pltpu.roll(k, 64, 1)).astype(BF16)
        out_ref[2 * i + 1, top:] = jnp.where(left, pltpu.roll(q, 64, 1), k).astype(BF16)


def pack(own, queries, keys, positions, blocks, sub):
    rows, width = queries.shape
    lane = jnp.arange(128, dtype=jnp.int32)
    inv_freq = rope_base ** (-(lane % 32).astype(F32) * 2.0 / 64)
    angles = positions.astype(F32)[:, None] / rope_scale * inv_freq[None, :]
    cosine = jnp.cos(angles)
    sine = jnp.where(lane % 64 < 32, -1.0, 1.0)[None, :] * jnp.sin(angles)
    return pl.pallas_call(
        functools.partial(pack_kernel, blocks=blocks, sub=sub),
        out_shape=jax.ShapeDtypeStruct((width // 64, 4 // blocks * sub + rows, 128), BF16),
        compiler_params=pltpu.CompilerParams(vmem_limit_bytes=12 << 20),
        name="pack",
    )(own, queries, keys, cosine, sine)


def experts_kernel(where_ref, x_ref, w_ref, other_ref, out_ref, wt_ref, *, n_e, tok_dev):
    zs, units, sub, _ = w_ref.shape
    tiles = units // n_e
    tile, zl = where_ref[0], where_ref[1]

    @pl.when((pl.program_id(0) == 0) & (pl.program_id(1) == 0))
    def _():
        for e in range(n_e):
            own, other = (r[:, e * tiles + tile].reshape(zs * sub, 128).astype(F32) for r in (w_ref, other_ref))
            both = [jnp.where(zl == i, own, other).T.astype(BF16) for i in range(2)]
            wt_ref[pl.ds(e * 128, 128), :] = jnp.concatenate(both, axis=1)

    depth = 2 * zs * sub
    n = x_ref.shape[0]
    x = x_ref[:, :tok_dev, :].reshape(n * tok_dev, depth)
    lanes = depth // 128
    high = 64 // (lanes * lanes)
    gates = jnp.concatenate(
        [
            jnp.concatenate(
                [x_ref[i, tok_dev:, pl.ds(t * 128, 128)].astype(F32)[:high] for t in range(lanes)], axis=0
            )
            for i in range(n)
        ],
        axis=1,
    )
    gates = jnp.where(tile == 0, pick_rows(gates, 0, n_e), pick_rows(gates, 1, n_e))
    prod = lax.dot_general(wt_ref[...], x, NT, preferred_element_type=F32)
    acc = None
    for e in range(n_e):
        gate = jnp.concatenate(
            [jnp.broadcast_to(gates[h * n_e + e : h * n_e + e + 1, :], (64, n * tok_dev)) for h in range(2)],
            axis=0,
        )
        term = prod[e * 128 : (e + 1) * 128] * gate
        acc = term if acc is None else acc + term
    out_ref[0] = acc.astype(BF16)


def pick_rows(gates, core, n_e):
    return jnp.concatenate([gates[h * n_e : (h + 1) * n_e] for h in (core, 2 + core)], axis=0)


def experts(tile, zl, x, w, other, seqs, n_e, tok_dev):
    blocks, rows, depth = x.shape
    per_seq = blocks // seqs
    return pl.pallas_call(
        functools.partial(experts_kernel, n_e=n_e, tok_dev=tok_dev),
        grid_spec=pltpu.PrefetchScalarGridSpec(
            num_scalar_prefetch=1,
            grid=(seqs, per_seq // STEP),
            in_specs=[
                pl.BlockSpec((STEP, rows, depth), lambda s, t, _: (s * (per_seq // STEP) + t, 0, 0)),
                pl.BlockSpec(w.shape, lambda s, t, _: (0, 0, 0, 0)),
                pl.BlockSpec(w.shape, lambda s, t, _: (0, 0, 0, 0)),
            ],
            out_specs=pl.BlockSpec((1, 128, STEP * tok_dev), lambda s, t, _: (s, 0, t)),
            scratch_shapes=[pltpu.VMEM((n_e * 128, depth), BF16)],
        ),
        out_shape=jax.ShapeDtypeStruct((seqs, 128, per_seq * tok_dev), BF16),
        cost_estimate=pl.CostEstimate(
            flops=2 * blocks * tok_dev * depth * n_e * 128, bytes_accessed=6 << 20, transcendentals=0
        ),
        compiler_params=pltpu.CompilerParams(vmem_limit_bytes=24 << 20),
        name="experts",
    )(jnp.stack([tile, zl]), x, w, other)


STEP = 8
TILE = 256


def weights_kernel(qk_ref, out_ref, *, top):
    blocks, rows, _ = qk_ref.shape
    rows -= top
    length = blocks * rows
    qk = qk_ref[:, top:, :].reshape(length, 128)
    q, k = qk[:, :64], qk[:, 64:]
    for j in range(length // TILE):
        upto = (j + 1) * TILE
        scores = lax.dot_general(k[:upto], q[j * TILE : upto], NT, preferred_element_type=F32) * 0.125
        key = lax.broadcasted_iota(jnp.int32, scores.shape, 0)
        query = lax.broadcasted_iota(jnp.int32, scores.shape, 1) + j * TILE
        scores = jnp.where(key <= query, scores, -1e30)
        most = jnp.max(scores, axis=0, keepdims=True)
        expd = jnp.exp(scores - most)
        out_ref[j, :upto, :] = (expd / jnp.sum(expd, axis=0, keepdims=True)).astype(BF16)


def attention_weights(qk, top):
    blocks, rows, _ = qk.shape
    length = blocks * (rows - top)
    return pl.pallas_call(
        functools.partial(weights_kernel, top=top),
        out_shape=jax.ShapeDtypeStruct((length // TILE, length, TILE), BF16),
        cost_estimate=pl.CostEstimate(flops=1 << 30, bytes_accessed=4 << 20, transcendentals=1 << 20),
        compiler_params=pltpu.CompilerParams(vmem_limit_bytes=24 << 20),
        name="weights",
    )(qk)


def attend_kernel(part_ref, p_ref, out_ref):
    rows = out_ref.shape[2]
    total = part_ref[0].astype(F32)
    for i in range(1, part_ref.shape[0]):
        total = total + part_ref[i].astype(F32)
    values = total.astype(BF16)
    for j in range(p_ref.shape[0]):
        upto = (j + 1) * TILE
        got = jnp.dot(values[:, :upto], p_ref[j, :upto, :], preferred_element_type=F32).astype(BF16)
        for b in range(TILE // rows):
            out_ref[j * (TILE // rows) + b] = got[:, b * rows : (b + 1) * rows]


def attend(parts, weights, blocks, rows):
    return pl.pallas_call(
        attend_kernel,
        out_shape=jax.ShapeDtypeStruct((blocks, 64, rows), BF16),
        cost_estimate=pl.CostEstimate(flops=1 << 28, bytes_accessed=4 << 20, transcendentals=0),
        compiler_params=pltpu.CompilerParams(vmem_limit_bytes=16 << 20),
        name="attend",
    )(parts, weights)


def a2a(array, axes):
    return lax.all_to_all(array, axes, 0, 0, tiled=True)


def per_device(tokens, queries, keys, positions, routes, router, value_experts):
    tok_dev, width = tokens.shape
    heads = routes.shape[0]
    n_exp = router.shape[1] // heads
    yh, yl = lax.axis_size("yh"), lax.axis_size("yl")
    seqs, cores = lax.axis_size("x"), lax.axis_size("c")
    group = ("yh", "yl", "c")
    plane = ("x",) + group
    fine = yl * cores
    own = value_experts[0]
    sub = own.shape[0] // fine
    cols = own.shape[1] // yh
    hb = heads // yh

    tiles = cols // 128
    top = tiles * sub
    got = a2a(pack(own, queries, keys, positions, yh, sub), group)
    logits = lax.dot_general(router, tokens, (((0,), (1,)), ((), ())), preferred_element_type=F32)
    ids = jnp.arange(n_exp, dtype=jnp.int32)
    named = jnp.any(routes[:, None, :, :] == ids[None, :, None, None], axis=-1)
    gates = jnp.where(named.reshape(heads * n_exp, tok_dev), jax.nn.sigmoid(logits), 0.0)
    got, sent = lax.optimization_barrier((got, regroup(tokens, gates, sub, yh)))
    x = a2a(sent, plane)

    mine = got[:, :top].reshape(n_exp * tiles, sub, 128)
    w = lax.all_gather(mine, "zh", axis=0)
    other = lax.ppermute(w, "zl", [(0, 1), (1, 0)])

    core, zl = lax.axis_index("c").astype(jnp.int32), lax.axis_index("zl").astype(jnp.int32)
    given = lax.ppermute(experts(1 - core, zl, x, w, other, seqs, n_exp, tok_dev), "c", [(0, 1), (1, 0)])
    kept = experts(core, zl, x, w, other, seqs, n_exp, tok_dev)
    partial = (kept.astype(F32) + given.astype(F32)).astype(BF16)
    parts = a2a(partial.reshape(seqs * yl, 64, partial.shape[2]), ("x", "yl"))
    out = attend(parts, attention_weights(got, top), got.shape[0], tok_dev)
    out = a2a(out, group)
    return out.reshape(heads * 64, tok_dev).T


def solution(mesh):
    fold = Mesh(mesh.devices.reshape(8, 2, 4, BLOCKS, 4 // BLOCKS, 2), ("zh", "zl", "x", "yh", "yl", "c"))
    rows = ("zh", "zl", "x", "yh", "yl", "c")
    placed = (
        P(rows, None),
        P(rows, None),
        P(rows, None),
        P(rows),
        P(None, rows, None),
        P(),
        P(("yh", "yl", "c"), ("zh", "zl", "x"), None),
    )
    return jax.shard_map(per_device, mesh=fold, in_specs=placed, out_specs=P(rows, None), check_vma=False)
```

```python
import functools

import jax
import jax.numpy as jnp
from jax import lax
from jax.experimental import pallas as pl
from jax.experimental.pallas import tpu as pltpu
from jax.sharding import Mesh
from jax.sharding import PartitionSpec as P


rope_base = 500000.0
rope_scale = 8.0
F32, BF16 = jnp.float32, jnp.bfloat16
NT = (((1,), (1,)), ((), ()))

BLOCKS = 2


def gate_rows(blocks):
    return max(64 // (blocks * blocks), 16)


def regroup_kernel(tok_ref, gate_ref, out_ref, *, sub, blocks):
    rows = tok_ref.shape[0]
    per = 128 // sub
    fine = 64 // sub
    depth = per * 128
    row = lax.broadcasted_iota(jnp.int32, (depth, 128), 0)
    col = lax.broadcasted_iota(jnp.int32, (depth, 128), 1)
    for half in range(2):
        for slot in range(per):
            pick = (row // 128 == col // sub) & (row % 128 == slot * sub + col % sub)
            pick = jnp.where(pick, 1.0, 0.0).astype(BF16)
            seq, part_of = divmod(half * per + slot, fine)
            for part in range(16 // per):
                cat = jnp.concatenate(
                    [tok_ref[:, pl.ds((i * (16 // per) + part) * 256 + half * 128, 128)] for i in range(per)], axis=1
                )
                got = jnp.dot(cat, pick, preferred_element_type=F32).astype(BF16)
                for block in range(blocks):
                    out_ref[(seq * blocks + block) * fine + part_of, :rows, pl.ds(part * 128, 128)] = got
    high = gate_ref.shape[0] // (blocks * blocks)
    for block in range(blocks):
        for tile in range(blocks):
            mine = gate_ref[pl.ds((block * blocks + tile) * high, high), :].astype(BF16)
            for seq in range(4):
                for part_of in range(fine):
                    spot = (seq * blocks + block) * fine + part_of
                    out_ref[spot, rows : rows + high, pl.ds(tile * 128, 128)] = mine
                    if high < out_ref.shape[1] - rows:
                        rest = jnp.zeros((out_ref.shape[1] - rows - high, 128), BF16)
                        out_ref[spot, rows + high :, pl.ds(tile * 128, 128)] = rest


def regroup(tokens, gates, sub, blocks):
    rows, width = tokens.shape
    slices = 256 // sub
    shape = (slices * blocks, rows + gate_rows(blocks), width // slices)
    return pl.pallas_call(
        functools.partial(regroup_kernel, sub=sub, blocks=blocks),
        out_shape=jax.ShapeDtypeStruct(shape, BF16),
        cost_estimate=pl.CostEstimate(flops=1 << 31, bytes_accessed=4 << 20, transcendentals=0),
        compiler_params=pltpu.CompilerParams(vmem_limit_bytes=16 << 20),
        name="regroup",
    )(tokens, gates)


def pack_kernel(own_ref, q_ref, k_ref, cos_ref, sin_ref, out_ref, *, blocks, sub):
    cosine, sine = cos_ref[...], sin_ref[...]
    lane = lax.broadcasted_iota(jnp.int32, cosine.shape, 1)
    low = lane % 64 < 32
    left = lane < 64
    tiles = 4 // blocks
    fine = 64 // sub
    for block in range(blocks):
        first, second = (
            own_ref[:, pl.ds((block * tiles + i) * 128, 128)].astype(F32) for i in range(2)
        )
        near = left[: first.shape[0]]
        halves = (
            jnp.where(near, first, pltpu.roll(second, 64, 1)).astype(BF16),
            jnp.where(near, pltpu.roll(first, 64, 1), second).astype(BF16),
        )
        for part in range(fine):
            for i, half in enumerate(halves):
                out_ref[block * fine + part, pl.ds(i * sub, sub), :] = half[part * sub : (part + 1) * sub]

    def rot(tile):
        tile = tile.astype(F32)
        other = jnp.where(low, pltpu.roll(tile, 96, 1), pltpu.roll(tile, 32, 1))
        return (tile * cosine + other * sine).astype(BF16).astype(F32)

    top = tiles * sub
    for i in range(q_ref.shape[1] // 128):
        q = rot(q_ref[:, pl.ds(i * 128, 128)])
        k = rot(k_ref[:, pl.ds(i * 128, 128)])
        out_ref[2 * i, top:] = jnp.where(left, q, pltpu.roll(k, 64, 1)).astype(BF16)
        out_ref[2 * i + 1, top:] = jnp.where(left, pltpu.roll(q, 64, 1), k).astype(BF16)


def pack(own, queries, keys, positions, blocks, sub):
    rows, width = queries.shape
    lane = jnp.arange(128, dtype=jnp.int32)
    inv_freq = rope_base ** (-(lane % 32).astype(F32) * 2.0 / 64)
    angles = positions.astype(F32)[:, None] / rope_scale * inv_freq[None, :]
    cosine = jnp.cos(angles)
    sine = jnp.where(lane % 64 < 32, -1.0, 1.0)[None, :] * jnp.sin(angles)
    return pl.pallas_call(
        functools.partial(pack_kernel, blocks=blocks, sub=sub),
        out_shape=jax.ShapeDtypeStruct((width // 64, 4 // blocks * sub + rows, 128), BF16),
        name="pack",
    )(own, queries, keys, cosine, sine)


def experts_kernel(where_ref, x_ref, w_ref, other_ref, out_ref, wt_ref, *, n_e, tok_dev):
    zs, units, sub, _ = w_ref.shape
    tiles = units // n_e
    tile, zl = where_ref[0], where_ref[1]

    for e in range(n_e):
        own, other = (r[:, e * tiles + tile].reshape(zs * sub, 128).astype(F32) for r in (w_ref, other_ref))
        both = [jnp.where(zl == i, own, other).T.astype(BF16) for i in range(2)]
        wt_ref[pl.ds(e * 128, 128), :] = jnp.concatenate(both, axis=1)

    depth = 2 * zs * sub
    n = x_ref.shape[0]
    x = x_ref[:, :tok_dev, :].reshape(n * tok_dev, depth)
    lanes = depth // 128
    high = 64 // (lanes * lanes)
    gates = jnp.concatenate(
        [
            jnp.concatenate(
                [x_ref[i, tok_dev:, pl.ds(t * 128, 128)].astype(F32)[:high] for t in range(lanes)], axis=0
            )
            for i in range(n)
        ],
        axis=1,
    )
    gates = jnp.where(tile == 0, pick_rows(gates, 0, n_e), pick_rows(gates, 1, n_e))
    for first in range(0, n * tok_dev, CHUNK):
        seq, at = divmod(first, out_ref.shape[2])
        spot = pl.ds(at, CHUNK)
        prod = lax.dot_general(wt_ref[...], x[first : first + CHUNK], NT, preferred_element_type=F32)
        for h in range(2):
            acc = None
            for e in range(n_e):
                at = h * n_e + e
                term = prod[e * 128 + h * 64 : e * 128 + h * 64 + 64] * gates[at : at + 1, first : first + CHUNK]
                acc = term if acc is None else acc + term
            out_ref[seq, pl.ds(h * 64, 64), spot] = acc.astype(BF16)


def pick_rows(gates, core, n_e):
    return jnp.concatenate([gates[h * n_e : (h + 1) * n_e] for h in (core, 2 + core)], axis=0)


def experts(tile, zl, x, w, other, seqs, n_e, tok_dev):
    blocks, rows, depth = x.shape
    vmem = pl.BlockSpec(memory_space=pltpu.VMEM)
    return pl.pallas_call(
        functools.partial(experts_kernel, n_e=n_e, tok_dev=tok_dev),
        in_specs=[pl.BlockSpec(memory_space=pltpu.SMEM), vmem, vmem, vmem],
        out_specs=vmem,
        out_shape=jax.ShapeDtypeStruct((seqs, 128, blocks // seqs * tok_dev), BF16),
        scratch_shapes=[pltpu.VMEM((n_e * 128, depth), BF16)],
        cost_estimate=pl.CostEstimate(
            flops=2 * blocks * tok_dev * depth * n_e * 128, bytes_accessed=6 << 20, transcendentals=0
        ),
        compiler_params=pltpu.CompilerParams(vmem_limit_bytes=24 << 20),
        name="experts",
    )(jnp.stack([tile, zl]), x, w, other)


CHUNK = 256
TILE = 256


def attend_kernel(qk_ref, part_ref, out_ref, *, top):
    blocks, rows, _ = qk_ref.shape
    rows -= top
    length = blocks * rows
    qk = qk_ref[:, top:, :].reshape(length, 128)
    q, k = qk[:, :64], qk[:, 64:]
    total = part_ref[0].astype(F32)
    for i in range(1, part_ref.shape[0]):
        total = total + part_ref[i].astype(F32)
    values = total.astype(BF16)
    for j in range(length // TILE):
        upto = (j + 1) * TILE
        scores = lax.dot_general(k[:upto], q[j * TILE : upto], NT, preferred_element_type=F32) * 0.125
        key = lax.broadcasted_iota(jnp.int32, scores.shape, 0)
        query = lax.broadcasted_iota(jnp.int32, scores.shape, 1) + j * TILE
        scores = jnp.where(key <= query, scores, -1e30)
        most = jnp.max(scores, axis=0, keepdims=True)
        expd = jnp.exp(scores - most)
        weights = (expd / jnp.sum(expd, axis=0, keepdims=True)).astype(BF16)
        got = jnp.dot(values[:, :upto], weights, preferred_element_type=F32).astype(BF16)
        for b in range(TILE // rows):
            out_ref[j * (TILE // rows) + b] = got[:, b * rows : (b + 1) * rows]


def attend(qk, parts, top):
    blocks, rows, _ = qk.shape
    return pl.pallas_call(
        functools.partial(attend_kernel, top=top),
        out_shape=jax.ShapeDtypeStruct((blocks, 64, rows - top), BF16),
        cost_estimate=pl.CostEstimate(flops=1 << 30, bytes_accessed=4 << 20, transcendentals=1 << 20),
        compiler_params=pltpu.CompilerParams(vmem_limit_bytes=24 << 20),
        name="attend",
    )(qk, parts)


def a2a(array, axes):
    return lax.all_to_all(array, axes, 0, 0, tiled=True)


def neighbours(zs, cores):
    pairs = []
    for z in range(zs):
        for core in range(cores):
            step = 1 if (z + core) % 2 == 0 else -1
            pairs.append((z * cores + core, (z + step) % zs * cores + core))
    return pairs


def per_device(tokens, queries, keys, positions, routes, router, value_experts):
    tok_dev, width = tokens.shape
    heads = routes.shape[0]
    n_exp = router.shape[1] // heads
    yh, yl = lax.axis_size("yh"), lax.axis_size("yl")
    seqs, cores = lax.axis_size("x"), lax.axis_size("c")
    group = ("yh", "yl", "c")
    plane = ("x",) + group
    fine = yl * cores
    own = value_experts[0]
    sub = own.shape[0] // fine
    cols = own.shape[1] // yh
    hb = heads // yh

    tiles = cols // 128
    top = tiles * sub
    got = a2a(pack(own, queries, keys, positions, yh, sub), group)
    logits = lax.dot_general(router, tokens, (((0,), (1,)), ((), ())), preferred_element_type=F32)
    ids = jnp.arange(n_exp, dtype=jnp.int32)
    named = jnp.any(routes[:, None, :, :] == ids[None, :, None, None], axis=-1)
    gates = jnp.where(named.reshape(heads * n_exp, tok_dev), jax.nn.sigmoid(logits), 0.0)
    got, sent = lax.optimization_barrier((got, regroup(tokens, gates, sub, yh)))
    x = a2a(sent, plane)

    mine = got[:, :top].reshape(n_exp * tiles, sub, 128)
    w = lax.all_gather(mine, "zh", axis=0)
    other = lax.ppermute(w, ("zh", "zl", "c"), neighbours(16, 2))

    core, zl = lax.axis_index("c").astype(jnp.int32), lax.axis_index("zl").astype(jnp.int32)
    given = lax.ppermute(experts(1 - core, zl, x, w, other, seqs, n_exp, tok_dev), "c", [(0, 1), (1, 0)])
    kept = experts(core, zl, x, w, other, seqs, n_exp, tok_dev)
    partial = (kept.astype(F32) + given.astype(F32)).astype(BF16)
    parts = a2a(partial.reshape(seqs * yl, 64, partial.shape[2]), ("x", "yl"))
    out = attend(got, parts, top)
    out = a2a(out, group)
    return out.reshape(heads * 64, tok_dev).T


def solution(mesh):
    fold = Mesh(mesh.devices.reshape(8, 2, 4, BLOCKS, 4 // BLOCKS, 2), ("zh", "zl", "x", "yh", "yl", "c"))
    rows = ("zh", "zl", "x", "yh", "yl", "c")
    placed = (
        P(rows, None),
        P(rows, None),
        P(rows, None),
        P(rows),
        P(None, rows, None),
        P(),
        P(("yh", "yl", "c"), ("zh", "zl", "x"), None),
    )
    return jax.shard_map(per_device, mesh=fold, in_specs=placed, out_specs=P(rows, None), check_vma=False)
```

```python
import functools

import jax
import jax.numpy as jnp
from jax import lax
from jax.experimental import pallas as pl
from jax.experimental.pallas import tpu as pltpu
from jax.sharding import Mesh
from jax.sharding import PartitionSpec as P


rope_base = 500000.0
rope_scale = 8.0
F32, BF16 = jnp.float32, jnp.bfloat16
NT = (((1,), (1,)), ((), ()))

BLOCKS = 2


def gate_rows(blocks):
    return max(64 // (blocks * blocks), 16)


def regroup_kernel(tok_ref, gate_ref, route_ref, out_ref, *, sub, blocks):
    rows = tok_ref.shape[0]
    per = 128 // sub
    fine = 64 // sub
    depth = per * 128
    row = lax.broadcasted_iota(jnp.int32, (depth, 128), 0)
    col = lax.broadcasted_iota(jnp.int32, (depth, 128), 1)
    for half in range(2):
        for slot in range(per):
            pick = (row // 128 == col // sub) & (row % 128 == slot * sub + col % sub)
            pick = jnp.where(pick, 1.0, 0.0).astype(BF16)
            seq, part_of = divmod(half * per + slot, fine)
            for part in range(16 // per):
                cat = jnp.concatenate(
                    [tok_ref[:, pl.ds((i * (16 // per) + part) * 256 + half * 128, 128)] for i in range(per)], axis=1
                )
                got = jnp.dot(cat, pick, preferred_element_type=F32).astype(BF16)
                for block in range(blocks):
                    out_ref[(seq * blocks + block) * fine + part_of, :rows, pl.ds(part * 128, 128)] = got
    heads = route_ref.shape[0]
    n_e = gate_ref.shape[0] // heads
    ids = lax.broadcasted_iota(jnp.int32, (n_e, rows), 0)
    gates = []
    for h in range(heads):
        named = (route_ref[h, 0:1, :] == ids) | (route_ref[h, 1:2, :] == ids)
        gates.append(jnp.where(named, gate_ref[pl.ds(h * n_e, n_e), :], 0.0))
    gates = jnp.concatenate(gates, axis=0)
    high = gates.shape[0] // (blocks * blocks)
    for block in range(blocks):
        for tile in range(blocks):
            mine = gates[(block * blocks + tile) * high : (block * blocks + tile + 1) * high].astype(BF16)
            for seq in range(4):
                for part_of in range(fine):
                    spot = (seq * blocks + block) * fine + part_of
                    out_ref[spot, rows : rows + high, pl.ds(tile * 128, 128)] = mine
                    if high < out_ref.shape[1] - rows:
                        rest = jnp.zeros((out_ref.shape[1] - rows - high, 128), BF16)
                        out_ref[spot, rows + high :, pl.ds(tile * 128, 128)] = rest


def regroup(tokens, gates, routes, sub, blocks):
    rows, width = tokens.shape
    slices = 256 // sub
    shape = (slices * blocks, rows + gate_rows(blocks), width // slices)
    return pl.pallas_call(
        functools.partial(regroup_kernel, sub=sub, blocks=blocks),
        out_shape=jax.ShapeDtypeStruct(shape, BF16),
        cost_estimate=pl.CostEstimate(flops=1 << 31, bytes_accessed=4 << 20, transcendentals=0),
        compiler_params=pltpu.CompilerParams(vmem_limit_bytes=16 << 20),
        name="regroup",
    )(tokens, gates, routes)


def pack_kernel(own_ref, q_ref, k_ref, pos_ref, freq_ref, out_ref, *, blocks, sub):
    rows = q_ref.shape[0]
    lane = lax.broadcasted_iota(jnp.int32, (rows, 128), 1)
    low = lane % 64 < 32
    left = lane < 64
    angles = jnp.broadcast_to(pos_ref[...].astype(F32), (128, rows)).T / rope_scale * freq_ref[...]
    cosine = jnp.cos(angles)
    sine = jnp.sin(angles)
    sine = jnp.where(low, -sine, sine)
    tiles = 4 // blocks
    fine = 64 // sub
    for block in range(blocks):
        first, second = (
            own_ref[:, pl.ds((block * tiles + i) * 128, 128)].astype(F32) for i in range(2)
        )
        near = left[: first.shape[0]]
        halves = (
            jnp.where(near, first, pltpu.roll(second, 64, 1)).astype(BF16),
            jnp.where(near, pltpu.roll(first, 64, 1), second).astype(BF16),
        )
        for part in range(fine):
            for i, half in enumerate(halves):
                out_ref[block * fine + part, pl.ds(i * sub, sub), :] = half[part * sub : (part + 1) * sub]

    def rot(tile):
        tile = tile.astype(F32)
        other = jnp.where(low, pltpu.roll(tile, 96, 1), pltpu.roll(tile, 32, 1))
        return (tile * cosine + other * sine).astype(BF16).astype(F32)

    top = tiles * sub
    for i in range(q_ref.shape[1] // 128):
        q = rot(q_ref[:, pl.ds(i * 128, 128)])
        k = rot(k_ref[:, pl.ds(i * 128, 128)])
        out_ref[2 * i, top:] = jnp.where(left, q, pltpu.roll(k, 64, 1)).astype(BF16)
        out_ref[2 * i + 1, top:] = jnp.where(left, pltpu.roll(q, 64, 1), k).astype(BF16)


def pack(own, queries, keys, positions, blocks, sub):
    rows, width = queries.shape
    lane = jnp.arange(128, dtype=jnp.int32)
    inv_freq = rope_base ** (-(lane % 32).astype(F32) * 2.0 / 64)
    return pl.pallas_call(
        functools.partial(pack_kernel, blocks=blocks, sub=sub),
        out_shape=jax.ShapeDtypeStruct((width // 64, 4 // blocks * sub + rows, 128), BF16),
        name="pack",
    )(own, queries, keys, positions.reshape(1, rows), inv_freq.reshape(1, 128))


def experts_kernel(where_ref, x_ref, w_ref, other_ref, out_ref, wt_ref, *, n_e, tok_dev):
    zs, units, sub, _ = w_ref.shape
    tiles = units // n_e
    tile, zl = where_ref[0], where_ref[1]

    for e in range(n_e):
        own, other = (r[:, e * tiles + tile].reshape(zs * sub, 128).astype(F32) for r in (w_ref, other_ref))
        both = [jnp.where(zl == i, own, other).T.astype(BF16) for i in range(2)]
        wt_ref[pl.ds(e * 128, 128), :] = jnp.concatenate(both, axis=1)

    depth = 2 * zs * sub
    n = x_ref.shape[0]
    x = x_ref[:, :tok_dev, :].reshape(n * tok_dev, depth)
    lanes = depth // 128
    high = 64 // (lanes * lanes)
    gates = jnp.concatenate(
        [
            jnp.concatenate(
                [x_ref[i, tok_dev:, pl.ds(t * 128, 128)].astype(F32)[:high] for t in range(lanes)], axis=0
            )
            for i in range(n)
        ],
        axis=1,
    )
    gates = jnp.where(tile == 0, pick_rows(gates, 0, n_e), pick_rows(gates, 1, n_e))
    for first in range(0, n * tok_dev, CHUNK):
        seq, at = divmod(first, out_ref.shape[2])
        spot = pl.ds(at, CHUNK)
        prod = lax.dot_general(wt_ref[...], x[first : first + CHUNK], NT, preferred_element_type=F32)
        for h in range(2):
            acc = None
            for e in range(n_e):
                at = h * n_e + e
                term = prod[e * 128 + h * 64 : e * 128 + h * 64 + 64] * gates[at : at + 1, first : first + CHUNK]
                acc = term if acc is None else acc + term
            out_ref[seq, pl.ds(h * 64, 64), spot] = acc.astype(BF16)


def pick_rows(gates, core, n_e):
    return jnp.concatenate([gates[h * n_e : (h + 1) * n_e] for h in (core, 2 + core)], axis=0)


def experts(tile, zl, x, w, other, seqs, n_e, tok_dev):
    blocks, rows, depth = x.shape
    vmem = pl.BlockSpec(memory_space=pltpu.VMEM)
    return pl.pallas_call(
        functools.partial(experts_kernel, n_e=n_e, tok_dev=tok_dev),
        in_specs=[pl.BlockSpec(memory_space=pltpu.SMEM), vmem, vmem, vmem],
        out_specs=vmem,
        out_shape=jax.ShapeDtypeStruct((seqs, 128, blocks // seqs * tok_dev), BF16),
        scratch_shapes=[pltpu.VMEM((n_e * 128, depth), BF16)],
        cost_estimate=pl.CostEstimate(
            flops=2 * blocks * tok_dev * depth * n_e * 128, bytes_accessed=6 << 20, transcendentals=0
        ),
        compiler_params=pltpu.CompilerParams(vmem_limit_bytes=24 << 20),
        name="experts",
    )(jnp.stack([tile, zl]), x, w, other)


CHUNK = 256
TILE = 256


def attend_kernel(qk_ref, part_ref, out_ref, *, top):
    blocks, rows, _ = qk_ref.shape
    rows -= top
    length = blocks * rows
    qk = qk_ref[:, top:, :].reshape(length, 128)
    q, k = qk[:, :64], qk[:, 64:]
    total = part_ref[0].astype(F32)
    for i in range(1, part_ref.shape[0]):
        total = total + part_ref[i].astype(F32)
    values = total.astype(BF16)
    for j in range(length // TILE):
        upto = (j + 1) * TILE
        scores = lax.dot_general(k[:upto], q[j * TILE : upto], NT, preferred_element_type=F32) * 0.125
        key = lax.broadcasted_iota(jnp.int32, (TILE, TILE), 0)
        query = lax.broadcasted_iota(jnp.int32, (TILE, TILE), 1)
        last = jnp.where(key <= query, scores[j * TILE :], -1e30)
        scores = last if j == 0 else jnp.concatenate([scores[: j * TILE], last], axis=0)
        most = jnp.max(scores, axis=0, keepdims=True)
        expd = jnp.exp(scores - most)
        weights = (expd * (1.0 / jnp.sum(expd, axis=0, keepdims=True))).astype(BF16)
        got = jnp.dot(values[:, :upto], weights, preferred_element_type=F32).astype(BF16)
        for b in range(TILE // rows):
            out_ref[j * (TILE // rows) + b] = got[:, b * rows : (b + 1) * rows]


def attend(qk, parts, top):
    blocks, rows, _ = qk.shape
    return pl.pallas_call(
        functools.partial(attend_kernel, top=top),
        out_shape=jax.ShapeDtypeStruct((blocks, 64, rows - top), BF16),
        cost_estimate=pl.CostEstimate(flops=1 << 30, bytes_accessed=4 << 20, transcendentals=1 << 20),
        compiler_params=pltpu.CompilerParams(vmem_limit_bytes=24 << 20),
        name="attend",
    )(qk, parts)


def a2a(array, axes):
    return lax.all_to_all(array, axes, 0, 0, tiled=True)


def neighbours(zs, cores):
    pairs = []
    for z in range(zs):
        for core in range(cores):
            step = 1 if (z + core) % 2 == 0 else -1
            pairs.append((z * cores + core, (z + step) % zs * cores + core))
    return pairs


def per_device(tokens, queries, keys, positions, routes, router, value_experts):
    tok_dev, width = tokens.shape
    heads = routes.shape[0]
    n_exp = router.shape[1] // heads
    yh, yl = lax.axis_size("yh"), lax.axis_size("yl")
    seqs, cores = lax.axis_size("x"), lax.axis_size("c")
    group = ("yh", "yl", "c")
    plane = ("x",) + group
    fine = yl * cores
    own = value_experts[0]
    sub = own.shape[0] // fine
    cols = own.shape[1] // yh
    hb = heads // yh

    tiles = cols // 128
    top = tiles * sub
    got = a2a(pack(own, queries, keys, positions, yh, sub), group)
    logits = lax.dot_general(router, tokens, (((0,), (1,)), ((), ())), preferred_element_type=F32)
    gates = jax.nn.sigmoid(logits)
    got, sent = lax.optimization_barrier((got, regroup(tokens, gates, routes.transpose(0, 2, 1), sub, yh)))
    x = a2a(sent, plane)

    mine = got[:, :top].reshape(n_exp * tiles, sub, 128)
    w = lax.all_gather(mine, "zh", axis=0)
    other = lax.ppermute(w, ("zh", "zl", "c"), neighbours(16, 2))

    core, zl = lax.axis_index("c").astype(jnp.int32), lax.axis_index("zl").astype(jnp.int32)
    given = lax.ppermute(experts(1 - core, zl, x, w, other, seqs, n_exp, tok_dev), "c", [(0, 1), (1, 0)])
    kept = experts(core, zl, x, w, other, seqs, n_exp, tok_dev)
    partial = (kept.astype(F32) + given.astype(F32)).astype(BF16)
    parts = a2a(partial.reshape(seqs * yl, 64, partial.shape[2]), ("x", "yl"))
    out = attend(got, parts, top)
    out = a2a(out, group)
    return out.reshape(heads * 64, tok_dev).T


def solution(mesh):
    fold = Mesh(mesh.devices.reshape(8, 2, 4, BLOCKS, 4 // BLOCKS, 2), ("zh", "zl", "x", "yh", "yl", "c"))
    rows = ("zh", "zl", "x", "yh", "yl", "c")
    placed = (
        P(rows, None),
        P(rows, None),
        P(rows, None),
        P(rows),
        P(None, rows, None),
        P(),
        P(("yh", "yl", "c"), ("zh", "zl", "x"), None),
    )
    return jax.shard_map(per_device, mesh=fold, in_specs=placed, out_specs=P(rows, None), check_vma=False)
```

```python
import functools

import jax
import jax.numpy as jnp
from jax import lax
from jax.experimental import pallas as pl
from jax.experimental.pallas import tpu as pltpu
from jax.sharding import Mesh
from jax.sharding import PartitionSpec as P


rope_base = 500000.0
rope_scale = 8.0
F32, BF16 = jnp.float32, jnp.bfloat16
NT = (((1,), (1,)), ((), ()))

BLOCKS = 2


def gate_rows(blocks):
    return max(64 // (blocks * blocks), 16)


def regroup_kernel(tok_ref, gate_ref, route_ref, out_ref, *, sub, blocks):
    rows = tok_ref.shape[0]
    per = 128 // sub
    fine = 64 // sub
    depth = per * 128
    row = lax.broadcasted_iota(jnp.int32, (depth, 128), 0)
    col = lax.broadcasted_iota(jnp.int32, (depth, 128), 1)
    for half in range(2):
        for slot in range(per):
            pick = (row // 128 == col // sub) & (row % 128 == slot * sub + col % sub)
            pick = jnp.where(pick, 1.0, 0.0).astype(BF16)
            seq, part_of = divmod(half * per + slot, fine)
            for part in range(16 // per):
                cat = jnp.concatenate(
                    [tok_ref[:, pl.ds((i * (16 // per) + part) * 256 + half * 128, 128)] for i in range(per)], axis=1
                )
                got = jnp.dot(cat, pick, preferred_element_type=F32).astype(BF16)
                for block in range(blocks):
                    out_ref[(seq * blocks + block) * fine + part_of, :rows, pl.ds(part * 128, 128)] = got
    heads = route_ref.shape[0]
    n_e = gate_ref.shape[0] // heads
    ids = lax.broadcasted_iota(jnp.int32, (n_e, rows), 0)
    gates = []
    for h in range(heads):
        named = (route_ref[h, 0:1, :] == ids) | (route_ref[h, 1:2, :] == ids)
        gates.append(jnp.where(named, gate_ref[pl.ds(h * n_e, n_e), :], 0.0))
    gates = jnp.concatenate(gates, axis=0)
    high = gates.shape[0] // (blocks * blocks)
    for block in range(blocks):
        for tile in range(blocks):
            mine = gates[(block * blocks + tile) * high : (block * blocks + tile + 1) * high].astype(BF16)
            for seq in range(4):
                for part_of in range(fine):
                    spot = (seq * blocks + block) * fine + part_of
                    out_ref[spot, rows : rows + high, pl.ds(tile * 128, 128)] = mine
                    if high < out_ref.shape[1] - rows:
                        rest = jnp.zeros((out_ref.shape[1] - rows - high, 128), BF16)
                        out_ref[spot, rows + high :, pl.ds(tile * 128, 128)] = rest


def regroup(tokens, gates, routes, sub, blocks):
    rows, width = tokens.shape
    slices = 256 // sub
    shape = (slices * blocks, rows + gate_rows(blocks), width // slices)
    return pl.pallas_call(
        functools.partial(regroup_kernel, sub=sub, blocks=blocks),
        out_shape=jax.ShapeDtypeStruct(shape, BF16),
        cost_estimate=pl.CostEstimate(flops=1 << 31, bytes_accessed=4 << 20, transcendentals=0),
        compiler_params=pltpu.CompilerParams(vmem_limit_bytes=16 << 20),
        name="regroup",
    )(tokens, gates, routes)


def pack_kernel(own_ref, q_ref, k_ref, pos_ref, freq_ref, out_ref, *, blocks, sub):
    rows = q_ref.shape[0]
    lane = lax.broadcasted_iota(jnp.int32, (rows, 128), 1)
    low = lane % 64 < 32
    left = lane < 64
    angles = jnp.broadcast_to(pos_ref[...].astype(F32), (128, rows)).T / rope_scale * freq_ref[...]
    cosine = jnp.cos(angles)
    sine = jnp.sin(angles)
    sine = jnp.where(low, -sine, sine)
    tiles = 4 // blocks
    fine = 64 // sub
    for block in range(blocks):
        first, second = (
            own_ref[:, pl.ds((block * tiles + i) * 128, 128)].astype(F32) for i in range(2)
        )
        near = left[: first.shape[0]]
        halves = (
            jnp.where(near, first, pltpu.roll(second, 64, 1)).astype(BF16),
            jnp.where(near, pltpu.roll(first, 64, 1), second).astype(BF16),
        )
        for part in range(fine):
            for i in range(2):
                half = halves[(part + 1 + i) % 2]
                out_ref[block * fine + part, pl.ds(i * sub, sub), :] = half[part * sub : (part + 1) * sub]

    def rot(tile):
        tile = tile.astype(F32)
        other = jnp.where(low, pltpu.roll(tile, 96, 1), pltpu.roll(tile, 32, 1))
        return (tile * cosine + other * sine).astype(BF16).astype(F32)

    top = tiles * sub
    for i in range(q_ref.shape[1] // 128):
        q = rot(q_ref[:, pl.ds(i * 128, 128)])
        k = rot(k_ref[:, pl.ds(i * 128, 128)])
        out_ref[2 * i, top:] = jnp.where(left, q, pltpu.roll(k, 64, 1)).astype(BF16)
        out_ref[2 * i + 1, top:] = jnp.where(left, pltpu.roll(q, 64, 1), k).astype(BF16)


def pack(own, queries, keys, positions, blocks, sub):
    rows, width = queries.shape
    lane = jnp.arange(128, dtype=jnp.int32)
    inv_freq = rope_base ** (-(lane % 32).astype(F32) * 2.0 / 64)
    return pl.pallas_call(
        functools.partial(pack_kernel, blocks=blocks, sub=sub),
        out_shape=jax.ShapeDtypeStruct((width // 64, 4 // blocks * sub + rows, 128), BF16),
        name="pack",
    )(own, queries, keys, positions.reshape(1, rows), inv_freq.reshape(1, 128))


def experts_kernel(where_ref, x_ref, w_ref, other_ref, out_ref, wt_ref, *, n_e, tok_dev):
    zs, _, sub, _ = w_ref.shape
    tile, zl = where_ref[0], where_ref[1]

    for e in range(n_e):
        own, other = (r[:, e].reshape(zs * sub, 128).astype(F32) for r in (w_ref, other_ref))
        both = [jnp.where(zl == i, own, other).T.astype(BF16) for i in range(2)]
        wt_ref[pl.ds(e * 128, 128), :] = jnp.concatenate(both, axis=1)

    depth = 2 * zs * sub
    n = x_ref.shape[0]
    x = x_ref[:, :tok_dev, :].reshape(n * tok_dev, depth)
    lanes = depth // 128
    high = 64 // (lanes * lanes)
    gates = jnp.concatenate(
        [
            jnp.concatenate(
                [x_ref[i, tok_dev:, pl.ds(t * 128, 128)].astype(F32)[:high] for t in range(lanes)], axis=0
            )
            for i in range(n)
        ],
        axis=1,
    )
    gates = jnp.where(tile == 0, pick_rows(gates, 0, n_e), pick_rows(gates, 1, n_e))
    for first in range(0, n * tok_dev, CHUNK):
        seq, at = divmod(first, out_ref.shape[2])
        spot = pl.ds(at, CHUNK)
        prod = lax.dot_general(wt_ref[...], x[first : first + CHUNK], NT, preferred_element_type=F32)
        for h in range(2):
            acc = None
            for e in range(n_e):
                at = h * n_e + e
                term = prod[e * 128 + h * 64 : e * 128 + h * 64 + 64] * gates[at : at + 1, first : first + CHUNK]
                acc = term if acc is None else acc + term
            out_ref[seq, pl.ds(h * 64, 64), spot] = acc.astype(BF16)


def pick_rows(gates, core, n_e):
    return jnp.concatenate([gates[h * n_e : (h + 1) * n_e] for h in (core, 2 + core)], axis=0)


def experts(tile, zl, x, w, other, seqs, n_e, tok_dev):
    blocks, _, depth = x.shape
    vmem = pl.BlockSpec(memory_space=pltpu.VMEM)
    return pl.pallas_call(
        functools.partial(experts_kernel, n_e=n_e, tok_dev=tok_dev),
        in_specs=[pl.BlockSpec(memory_space=pltpu.SMEM), vmem, vmem, vmem],
        out_specs=vmem,
        out_shape=jax.ShapeDtypeStruct((seqs, 128, blocks // seqs * tok_dev), BF16),
        scratch_shapes=[pltpu.VMEM((n_e * 128, depth), BF16)],
        cost_estimate=pl.CostEstimate(
            flops=2 * blocks * tok_dev * depth * n_e * 128, bytes_accessed=6 << 20, transcendentals=0
        ),
        compiler_params=pltpu.CompilerParams(vmem_limit_bytes=24 << 20),
        name="experts",
    )(jnp.stack([tile, zl]), x, w, other)


CHUNK = 256
TILE = 256


def attend_kernel(qk_ref, part_ref, out_ref, *, top):
    blocks, rows, _ = qk_ref.shape
    rows -= top
    length = blocks * rows
    qk = qk_ref[:, top:, :].reshape(length, 128)
    q, k = qk[:, :64], qk[:, 64:]
    total = part_ref[0].astype(F32)
    for i in range(1, part_ref.shape[0]):
        total = total + part_ref[i].astype(F32)
    values = total.astype(BF16)
    for j in range(length // TILE):
        upto = (j + 1) * TILE
        scores = lax.dot_general(k[:upto], q[j * TILE : upto], NT, preferred_element_type=F32) * 0.125
        key = lax.broadcasted_iota(jnp.int32, (TILE, TILE), 0)
        query = lax.broadcasted_iota(jnp.int32, (TILE, TILE), 1)
        last = jnp.where(key <= query, scores[j * TILE :], -1e30)
        scores = last if j == 0 else jnp.concatenate([scores[: j * TILE], last], axis=0)
        most = jnp.max(scores, axis=0, keepdims=True)
        expd = jnp.exp(scores - most)
        weights = (expd * (1.0 / jnp.sum(expd, axis=0, keepdims=True))).astype(BF16)
        got = jnp.dot(values[:, :upto], weights, preferred_element_type=F32).astype(BF16)
        for b in range(TILE // rows):
            out_ref[j * (TILE // rows) + b] = got[:, b * rows : (b + 1) * rows]


def attend(qk, parts, top):
    blocks, rows, _ = qk.shape
    return pl.pallas_call(
        functools.partial(attend_kernel, top=top),
        out_shape=jax.ShapeDtypeStruct((blocks, 64, rows - top), BF16),
        cost_estimate=pl.CostEstimate(flops=1 << 30, bytes_accessed=4 << 20, transcendentals=1 << 20),
        compiler_params=pltpu.CompilerParams(vmem_limit_bytes=24 << 20),
        name="attend",
    )(qk, parts)


def a2a(array, axes):
    return lax.all_to_all(array, axes, 0, 0, tiled=True)


def neighbours(zs, cores):
    pairs = []
    for z in range(zs):
        for core in range(cores):
            step = 1 if (z + core) % 2 == 0 else -1
            pairs.append((z * cores + core, (z + step) % zs * cores + core))
    return pairs


def per_device(tokens, queries, keys, positions, routes, router, value_experts):
    tok_dev, _ = tokens.shape
    heads = routes.shape[0]
    n_exp = router.shape[1] // heads
    yh, yl = lax.axis_size("yh"), lax.axis_size("yl")
    seqs, cores = lax.axis_size("x"), lax.axis_size("c")
    group = ("yh", "yl", "c")
    plane = ("x",) + group
    fine = yl * cores
    own = value_experts[0]
    sub = own.shape[0] // fine
    cols = own.shape[1] // yh

    tiles = cols // 128
    top = tiles * sub
    got = a2a(pack(own, queries, keys, positions, yh, sub), group)
    logits = lax.dot_general(router, tokens, (((0,), (1,)), ((), ())), preferred_element_type=F32)
    gates = jax.nn.sigmoid(logits)
    got, sent = lax.optimization_barrier((got, regroup(tokens, gates, routes.transpose(0, 2, 1), sub, yh)))
    x = a2a(sent, plane)

    mine = got[:, :top].reshape(n_exp, tiles, sub, 128).transpose(1, 0, 2, 3)
    w = lax.all_gather(mine, "zh", axis=1)
    other = []
    for i in range(2):
        other.append(lax.ppermute(w[i], ("zh", "zl", "c"), neighbours(16, 2)))

    core, zl = lax.axis_index("c").astype(jnp.int32), lax.axis_index("zl").astype(jnp.int32)
    given = experts(1 - core, zl, x, w[0], other[0], seqs, n_exp, tok_dev)
    given = lax.ppermute(given, "c", [(0, 1), (1, 0)])
    kept = experts(core, zl, x, w[1], other[1], seqs, n_exp, tok_dev)
    partial = (kept.astype(F32) + given.astype(F32)).astype(BF16)
    parts = a2a(partial.reshape(seqs * yl, 64, partial.shape[2]), ("x", "yl"))
    out = attend(got, parts, top)
    out = a2a(out, group)
    return out.reshape(heads * 64, tok_dev).T


def solution(mesh):
    fold = Mesh(mesh.devices.reshape(8, 2, 4, BLOCKS, 4 // BLOCKS, 2), ("zh", "zl", "x", "yh", "yl", "c"))
    rows = ("zh", "zl", "x", "yh", "yl", "c")
    placed = (
        P(rows, None),
        P(rows, None),
        P(rows, None),
        P(rows),
        P(None, rows, None),
        P(),
        P(("yh", "yl", "c"), ("zh", "zl", "x"), None),
    )
    return jax.shard_map(per_device, mesh=fold, in_specs=placed, out_specs=P(rows, None), check_vma=False)
```
